256 devices in a mesh: shard: 32 (over x, z_hi, y), rep: 8 (over z_lo, core).
Axes of the slice: x: 4, y: 4, z: 8 (z_hi: 2, z_lo: 4; z = z_hi * 4 + z_lo), core: 2. Of those that a mesh axis runs over, the one named last changes fastest.
Arguments:
- momentum: bfloat16 [32, 512, 2048], P(None, 'shard'), may hold values from -6 to 6
- gradient: bfloat16 [32, 512, 2048], P(None, 'shard'), may hold values from -6 to 6
Outputs:
- new_momentum: bfloat16 [32, 512, 2048], P(None, 'shard')
- update: bfloat16 [32, 512, 2048], P(None, 'shard')
The draws below stay inside these ranges and needn't reach their ends.
All inputs are finite; a program needn't handle non-finite values.
Results may differ from the reference program's by a relative error of at most 0.00065.
The reference program's roundings to bfloat16 on the way (of `blended`) count: a program that leaves them out, or rounds other values in their place, can miss the bound.
Values may be sent and summed in bfloat16 or wider, within the bound.
A program may use at most 64 MiB of HBM per device.

```python
import jax
import jax.numpy as jnp
from jax import lax

ROWS = 512
COLS = 2048
ITERS = 5
EXPERTS = 32


def shard_levels(own_key, extent, pieces, low, high):
    def one(axis_at, shards_of):
        draws = jax.random.uniform(jax.random.fold_in(jax.random.fold_in(own_key, 6), axis_at), (shards_of,), jnp.float32, low / len(pieces), high / len(pieces))
        return jnp.repeat(jnp.exp(draws), extent[axis_at] // shards_of).reshape((-1,) + (1,) * (len(extent) - axis_at - 1))

    factor_of = one(*pieces[0])
    for cut in pieces[1:]:
        factor_of = factor_of * one(*cut)
    return factor_of


def normal_values(key, dims, spread, limit, pieces=(), dtype=jnp.bfloat16):
    entries = jax.random.normal(key, dims, jnp.float32) * spread
    if len(pieces) > 0:
        entries = shard_levels(key, dims, pieces, -0.22, 0.18) * entries
    return jnp.clip(entries, min=-limit, max=limit).astype(dtype)


def setup_inputs(seed: int = 0) -> dict:
    keys = jax.random.split(jax.random.key(seed), 3)
    momentum = normal_values(keys[0], (EXPERTS, ROWS, COLS), 1.0, 6.0, ((1, 32),))
    gradient = normal_values(keys[1], (EXPERTS, ROWS, COLS), 1.0, 6.0, ((1, 32),))
    return {"momentum": momentum, "gradient": gradient}


coef_a = 3.4445
coef_b = -4.775
coef_c = 2.0315

def orthogonal(matrix):
    values = matrix.astype(jnp.float32)
    norm_value = jnp.sqrt(jnp.sum(values * values)) + 1e-07
    iterate = values / norm_value
    for sweep in range(ITERS):
        gram_matrix = jnp.dot(iterate, iterate.T, precision=lax.Precision.HIGHEST)
        polynomial = coef_b * gram_matrix + coef_c * jnp.dot(gram_matrix, gram_matrix, precision=lax.Precision.HIGHEST)
        iterate = coef_a * iterate + jnp.dot(polynomial, iterate, precision=lax.Precision.HIGHEST)
    return (iterate * jnp.sqrt(jnp.float32(max(ROWS, COLS)))).astype(jnp.bfloat16)

def reference(momentum, gradient):
    new_momentum = (0.95 * momentum.astype(jnp.float32) + gradient.astype(jnp.float32)).astype(jnp.bfloat16)
    blended = (gradient.astype(jnp.float32) + 0.95 * new_momentum.astype(jnp.float32)).astype(jnp.bfloat16)
    update = lax.map(orthogonal, blended)
    return (new_momentum, update)
```

```python
import functools

import jax
import jax.numpy as jnp
from jax import lax
from jax.experimental import pallas as pl
from jax.experimental.pallas import tpu as pltpu
from jax.sharding import PartitionSpec as P

ROWS = 512
COLS = 2048
ITERS = 5
EXPERTS = 32

coef_a = 3.4445
coef_b = -4.775
coef_c = 2.0315

MESH = pl.DeviceIdType.MESH
F32 = jnp.float32
BF16 = jnp.bfloat16

BAND = ROWS // 32
HALF = COLS // 2
QUARTER = HALF // 4
SPAN = 2
CHUNKS = 16 // SPAN
PER_X = 4 // SPAN


def hop_order(step):
    return lax.rem(step + step // 2 - 2 * (step // 3), 4)


class Place:
    def __init__(self):
        self.s = lax.axis_index("shard")
        self.r = lax.axis_index("rep")
        self.x = self.s // 8
        self.h = (self.s // 4) % 2
        self.y = self.s % 4
        self.zl = self.r // 2
        self.c = self.r % 2
        self.flow = self.zl // 2
        self.entry = 3 * (1 - self.flow)
        self.col = pl.multiple_of(self.c * HALF, HALF)
        self.other_col = pl.multiple_of((1 - self.c) * HALF, HALF)

    def shard(self, x, h, y):
        return x * 8 + h * 4 + y

    def rep(self, zl):
        return zl * 2 + self.c


def greet(p):
    barrier = pltpu.get_barrier_semaphore()

    def signal(s, r):
        pl.semaphore_signal(barrier, inc=1, device_id=(s, r), device_id_type=MESH)

    def near(i, _):
        x, y = lax.rem(p.x + i // 4, 4), lax.rem(p.y + i % 4, 4)

        @pl.when(i > 0)
        def _():
            signal(p.shard(x, p.h, y), p.r)

        return 0

    def across(i, _):
        x, y = lax.rem(p.x + i // 4, 4), lax.rem(p.y + i % 4, 4)
        first = 2 * (1 - p.zl // 3)
        signal(p.shard(x, 1 - p.h, y), p.rep(first))
        signal(p.shard(x, 1 - p.h, y), p.rep(first + 1))
        return 0

    @pl.when((p.zl == 0) | (p.zl == 3))
    def _():
        lax.fori_loop(0, 16, across, 0)

    lax.fori_loop(0, 16, near, 0)
    signal(p.s, p.zl * 2 + 1 - p.c)

    @pl.when(p.zl < 3)
    def _():
        signal(p.s, p.rep(p.zl + 1))

    @pl.when(p.zl > 0)
    def _():
        signal(p.s, p.rep(p.zl - 1))


def await_greetings(p):
    inner = (p.zl * (3 - p.zl)) // 2
    pl.semaphore_wait(pltpu.get_barrier_semaphore(), 15 + 16 + 1 + 1 + inner)


class Exchange:
    def __init__(self, p, src, dst, direct, relayed, pair_direct, pair_relayed, sends):
        self.p, self.src, self.dst = p, src, dst
        self.direct, self.relayed = direct, relayed
        self.pair_direct, self.pair_relayed = pair_direct, pair_relayed
        self.sends = sends

    def send_across(self):
        p = self.p
        cols = pl.multiple_of(p.zl * QUARTER, QUARTER)
        into = pl.multiple_of(p.c * HALF + p.zl * QUARTER, QUARTER)
        chunk = p.x * PER_X + p.y // SPAN

        def one(i, _):
            x = lax.rem(p.x + hop_order(i // 4), 4)
            y = lax.rem(p.y + hop_order(i % 4), 4)
            to = p.shard(x, 1 - p.h, y)
            pltpu.make_async_remote_copy(
                src_ref=self.src.at[to, :, pl.ds(cols, QUARTER)],
                dst_ref=self.dst.at[p.s, :, pl.ds(into, QUARTER)],
                send_sem=self.sends.at[0],
                recv_sem=self.relayed.at[p.flow, chunk],
                device_id=(to, p.rep(p.entry)),
                device_id_type=MESH,
            ).start()
            return 0

        lax.fori_loop(0, 16, one, 0)

    def send_near(self):
        p = self.p

        def one(i, _):
            x = lax.rem(p.x + hop_order(i // 4), 4)
            y = lax.rem(p.y + hop_order(i % 4), 4)
            to = p.shard(x, p.h, y)

            @pl.when(i > 0)
            def _():
                pltpu.make_async_remote_copy(
                    src_ref=self.src.at[to],
                    dst_ref=self.dst.at[p.s, :, pl.ds(p.col, HALF)],
                    send_sem=self.sends.at[1],
                    recv_sem=self.direct.at[p.x],
                    device_id=(to, p.r),
                    device_id_type=MESH,
                ).start()

            return 0

        pltpu.make_async_copy(
            self.src.at[p.s],
            self.dst.at[p.s, :, pl.ds(p.col, HALF)],
            self.direct.at[p.x],
        ).start()
        lax.fori_loop(0, 16, one, 0)

    def flow_chunk(self, flow, k, half_col):
        p = self.p
        x = lax.rem(p.x + hop_order(k // PER_X), 4)
        part = k % PER_X
        slot = p.shard(x, 1 - p.h, part * SPAN)
        cols = pl.multiple_of(half_col + flow * 2 * QUARTER, 2 * QUARTER)
        at = self.dst.at[pl.ds(slot, SPAN), :, pl.ds(cols, 2 * QUARTER)]
        return at, x * PER_X + part

    def relay(self, flow, k, sink):
        p = self.p
        at, sem = self.flow_chunk(flow, k, p.c * HALF)
        pltpu.make_async_copy(at, at, self.relayed.at[flow, sem]).wait()
        more = (p.zl > 0) if flow == 0 else (p.zl < 3)

        @pl.when(more)
        def _():
            pltpu.make_async_remote_copy(
                src_ref=at,
                dst_ref=at,
                send_sem=self.sends.at[2 + flow],
                recv_sem=self.relayed.at[flow, sem],
                device_id=(p.s, p.rep(p.zl - 1 if flow == 0 else p.zl + 1)),
                device_id_type=MESH,
            ).start()

        pltpu.make_async_remote_copy(
            src_ref=at,
            dst_ref=at,
            send_sem=self.sends.at[4],
            recv_sem=self.pair_relayed.at[flow, sem],
            device_id=(p.s, p.zl * 2 + 1 - p.c),
            device_id_type=MESH,
        ).start()
        sink(at)

    def direct_group(self, g, half_col):
        p = self.p
        x = lax.rem(p.x + hop_order(g), 4)
        cols = pl.multiple_of(half_col, HALF)
        at = self.dst.at[pl.ds(p.shard(x, p.h, 0), 4), :, pl.ds(cols, HALF)]
        return at, x

    def pass_direct(self, g, sink):
        p = self.p
        at, x = self.direct_group(g, p.c * HALF)
        pltpu.make_async_copy(at, at, self.direct.at[x]).wait()
        pltpu.make_async_remote_copy(
            src_ref=at,
            dst_ref=at,
            send_sem=self.sends.at[5],
            recv_sem=self.pair_direct.at[x],
            device_id=(p.s, p.zl * 2 + 1 - p.c),
            device_id_type=MESH,
        ).start()
        sink(at)

    def gather(self, sink):
        p = self.p

        def step(t, _):
            for flow in (0, 1):
                k = t - (3 - p.zl if flow == 0 else p.zl)

                @pl.when((k >= 0) & (k < CHUNKS))
                def _():
                    self.relay(flow, k, sink)

            @pl.when(t >= CHUNKS - 1)
            def _():
                self.pass_direct(t - (CHUNKS - 1), sink)

            return 0

        lax.fori_loop(0, CHUNKS + 3, step, 0)

        def partner_direct(g, _):
            at, x = self.direct_group(g, (1 - p.c) * HALF)
            pltpu.make_async_copy(at, at, self.pair_direct.at[x]).wait()
            sink(at)
            return 0

        lax.fori_loop(0, 4, partner_direct, 0)

        def partner_relayed(k, _):
            for flow in (0, 1):
                at, sem = self.flow_chunk(flow, k, (1 - p.c) * HALF)
                pltpu.make_async_copy(at, at, self.pair_relayed.at[flow, sem]).wait()
                sink(at)
            return 0

        lax.fori_loop(0, CHUNKS, partner_relayed, 0)

    def finish_sends(self):
        p = self.p

        def drain(index, slots):
            of = self.src.at[pl.ds(0, slots)]
            pltpu.make_async_copy(of, of, self.sends.at[index]).wait()

        drain(0, 4)
        drain(1, 15)

        @pl.when(p.zl > 0)
        def _():
            drain(2, 8)

        @pl.when(p.zl < 3)
        def _():
            drain(3, 8)

        drain(4, 16)
        drain(5, 16)


def halves(value, high_ref, low_ref):
    high = value.astype(BF16)
    high_ref[...] = high
    low_ref[...] = (value - high.astype(F32)).astype(BF16)


def mul(lh, ll, rh, rl):
    dot = functools.partial(jnp.dot, preferred_element_type=F32)
    return dot(lh[...], rh[...]) + (dot(lh[...], rl[...]) + dot(ll[...], rh[...]))


def chain(x_ref, gram, q, ah, al, rh, rl, ch, cl, qh, ql):
    eye = lax.broadcasted_iota(jnp.int32, (ROWS, ROWS), 0) == lax.broadcasted_iota(
        jnp.int32, (ROWS, ROWS), 1
    )
    values = x_ref[...].reshape(ROWS, COLS)
    raw = lax.dot_general(
        values, values, (((1,), (1,)), ((), ())), preferred_element_type=F32
    )
    gram[...] = raw
    square = jnp.sum(jnp.where(eye, raw, 0.0), axis=(0, 1), keepdims=True)
    inverse = 1.0 / (jnp.sqrt(square) + 1e-07)
    gram[...] = gram[...] * inverse * inverse
    q[...] = jnp.where(eye, 1.0, 0.0)
    halves(q[...], qh, ql)

    def sweep(i, _):
        halves(gram[...], ah, al)
        poly = coef_b * gram[...] + coef_c * mul(ah, al, ah, al)
        halves(poly, rh, rl)
        q[...] = coef_a * q[...] + mul(rh, rl, qh, ql)
        halves(q[...], qh, ql)

        @pl.when(i < ITERS - 1)
        def _():
            gram[...] = coef_a * gram[...] + mul(rh, rl, ah, al)
            halves(gram[...], ch, cl)
            gram[...] = coef_a * gram[...] + mul(ch, cl, rh, rl)

        return 0

    lax.fori_loop(0, ITERS, sweep, 0)
    return inverse * jnp.sqrt(F32(max(ROWS, COLS)))


def kernel(
    mom, grad, new_mom, update, mv, gv, nv, sb, xb, yb, ob,
    gram, q, ah, al, rh, rl, ch, cl, qh, ql,
    load_sem, store_sem, direct, relayed, pair_direct, pair_relayed, sends,
):
    p = Place()
    greet(p)

    def load(index, src, dst, col):
        return pltpu.make_async_copy(
            src.at[:, :, pl.ds(col, HALF)],
            dst.at[:, :, pl.ds(col, HALF)],
            load_sem.at[index],
        )

    loads = [
        load(0, mom, mv, p.col),
        load(1, grad, gv, p.col),
        load(2, mom, mv, p.other_col),
        load(3, grad, gv, p.other_col),
    ]
    for copy in loads:
        copy.start()
    loads[0].wait()
    loads[1].wait()

    def momentum(e, col):
        cols = pl.ds(col, HALF)
        g = gv[e, :, cols].astype(F32)
        n = (0.95 * mv[e, :, cols].astype(F32) + g).astype(BF16)
        nv[e, :, cols] = n
        return n, g

    def blend(e, _):
        n, g = momentum(e, p.col)
        sb[e] = (g + 0.95 * n.astype(F32)).astype(BF16)
        return 0

    lax.fori_loop(0, EXPERTS, blend, 0)
    await_greetings(p)

    def exchange(phase, src, dst):
        return Exchange(
            p, src, dst, direct.at[phase], relayed.at[phase],
            pair_direct.at[phase], pair_relayed.at[phase], sends.at[phase],
        )

    inward = exchange(0, sb, xb)
    inward.send_across()
    inward.send_near()

    loads[2].wait()
    loads[3].wait()

    def rest(e, _):
        momentum(e, p.other_col)
        return 0

    lax.fori_loop(0, EXPERTS, rest, 0)
    store = pltpu.make_async_copy(nv, new_mom, store_sem.at[0])
    store.start()
    inward.gather(lambda at: None)

    factor = chain(xb, gram, q, ah, al, rh, rl, ch, cl, qh, ql)

    dot = functools.partial(jnp.dot, preferred_element_type=F32)

    def product(h, cols, width):
        rows = [pl.ds(pl.multiple_of(x * 128 + h * 64, 64), 64) for x in range(4)]
        high = jnp.concatenate([qh[i, :] for i in rows], 0)
        low = jnp.concatenate([ql[i, :] for i in rows], 0)
        values = xb[:, :, pl.ds(cols, width)].reshape(ROWS, width)
        return ((dot(high, values) + dot(low, values)) * factor).astype(BF16)

    outward = exchange(1, yb, ob)
    across = pl.multiple_of(p.c * HALF + p.zl * QUARTER, QUARTER)
    part = product(1 - p.h, across, QUARTER).reshape(4, 4, BAND, QUARTER)
    for x in range(4):
        slots = pl.ds(p.shard(x, 1 - p.h, 0), 4)
        yb[slots, :, pl.ds(pl.multiple_of(p.zl * QUARTER, QUARTER), QUARTER)] = part[x]
    outward.send_across()
    part = product(p.h, p.col, HALF).reshape(4, 4, BAND, HALF)
    for x in range(4):
        yb[pl.ds(p.shard(x, p.h, 0), 4)] = part[x]
    outward.send_near()
    outward.gather(lambda at: None)
    out = pltpu.make_async_copy(ob, update, store_sem.at[1])
    out.start()
    inward.finish_sends()
    outward.finish_sends()
    store.wait()
    out.wait()


def shards(momentum, gradient):
    whole = (EXPERTS, BAND, COLS)
    dma = pltpu.SemaphoreType.DMA
    square = (ROWS, ROWS)
    return pl.pallas_call(
        kernel,
        out_shape=(
            jax.ShapeDtypeStruct(whole, BF16),
            jax.ShapeDtypeStruct(whole, BF16),
        ),
        in_specs=[pl.BlockSpec(memory_space=pl.ANY)] * 2,
        out_specs=[pl.BlockSpec(memory_space=pl.ANY)] * 2,
        scratch_shapes=[
            pltpu.VMEM(whole, BF16),
            pltpu.VMEM(whole, BF16),
            pltpu.VMEM(whole, BF16),
            pltpu.VMEM((EXPERTS, BAND, HALF), BF16),
            pltpu.VMEM(whole, BF16),
            pltpu.VMEM((EXPERTS, BAND, HALF), BF16),
            pltpu.VMEM(whole, BF16),
            pltpu.VMEM(square, F32),
            pltpu.VMEM(square, F32),
        ]
        + [pltpu.VMEM(square, BF16)] * 8
        + [
            dma((4,)),
            dma((2,)),
            dma((2, 4)),
            dma((2, 2, CHUNKS)),
            dma((2, 4)),
            dma((2, 2, CHUNKS)),
            dma((2, 6)),
        ],
        compiler_params=pltpu.CompilerParams(
            collective_id=0,
            has_side_effects=True,
            vmem_limit_bytes=48 * 1024 * 1024,
        ),
    )(momentum, gradient)


def solution(mesh):
    return jax.shard_map(
        shards,
        mesh=mesh,
        in_specs=(P(None, "shard", None), P(None, "shard", None)),
        out_specs=(P(None, "shard", None), P(None, "shard", None)),
        check_vma=False,
    )
```

```python
import functools

import jax
import jax.numpy as jnp
from jax import lax
from jax.experimental import pallas as pl
from jax.experimental.pallas import tpu as pltpu
from jax.sharding import PartitionSpec as P

ROWS = 512
COLS = 2048
ITERS = 5
EXPERTS = 32

coef_a = 3.4445
coef_b = -4.775
coef_c = 2.0315

MESH = pl.DeviceIdType.MESH
F32 = jnp.float32
BF16 = jnp.bfloat16

BAND = ROWS // 32
HALF = COLS // 2
PART = COLS // 8
LAG = 4
NEAR_AT = 13


def hop_order(step):
    return lax.rem(step + step // 2 - 2 * (step // 3), 4)


class Place:
    def __init__(self):
        self.s = lax.axis_index("shard")
        self.r = lax.axis_index("rep")
        self.x = self.s // 8
        self.h = (self.s // 4) % 2
        self.y = self.s % 4
        self.zl = self.r // 2
        self.c = self.r % 2
        self.partner = self.zl * 2 + 1 - self.c
        self.hop = (1 - self.c) * (3 - self.zl) + self.c * self.zl
        self.before = self.r + 2 - 4 * self.c
        self.after = self.r - 2 + 4 * self.c
        self.first = 6 - 5 * (self.zl // 2)
        self.col = pl.multiple_of(self.c * HALF, HALF)
        self.other_col = pl.multiple_of((1 - self.c) * HALF, HALF)
        self.part = pl.multiple_of(self.r * PART, PART)

    def shard(self, x, h, y):
        return x * 8 + h * 4 + y

    def far(self, i):
        x = lax.rem(self.x + hop_order(i // 4), 4)
        y = lax.rem(self.y + hop_order(i % 4), 4)
        return self.shard(x, 1 - self.h, y)

    def near(self, i):
        x = lax.rem(self.x + hop_order(i // 4), 4)
        y = lax.rem(self.y + hop_order(i % 4), 4)
        return self.shard(x, self.h, y)


def greet(p):
    barrier = pltpu.get_barrier_semaphore()

    def signal(s, r):
        pl.semaphore_signal(barrier, inc=1, device_id=(s, r), device_id_type=MESH)

    def near(i, _):
        signal(p.near(i), p.r)
        return 0

    def across(i, _):
        for r in range(4):
            signal(p.far(i), 4 * p.c + r)
        return 0

    @pl.when(p.hop == 0)
    def _():
        lax.fori_loop(0, 16, across, 0)

    lax.fori_loop(1, 16, near, 0)
    signal(p.s, p.partner)

    @pl.when(p.hop > 0)
    def _():
        signal(p.s, p.before)


def await_greetings(p):
    pl.semaphore_wait(pltpu.get_barrier_semaphore(), 15 + 16 + 1 + 1 - p.hop // 3)


class Exchange:
    def __init__(self, p, src, far_src, dst, direct, relayed, pair_direct, pair_relayed, sends):
        self.p, self.src, self.far_src, self.dst = p, src, far_src, dst
        self.direct, self.relayed = direct, relayed
        self.pair_direct, self.pair_relayed = pair_direct, pair_relayed
        self.sends = sends

    def send(self, src, dst, send_sem, recv_sem, s, r):
        pltpu.make_async_remote_copy(
            src_ref=src,
            dst_ref=dst,
            send_sem=self.sends.at[send_sem],
            recv_sem=recv_sem,
            device_id=(s, r),
            device_id_type=MESH,
        ).start()

    def send_across(self):
        p = self.p

        def one(i, _):
            to = p.far(i)
            into = self.dst.at[p.s, :, pl.ds(p.part, PART)]
            self.send(self.far_src.at[to], into, 0, self.relayed.at[p.s], to, p.first)
            return 0

        lax.fori_loop(0, 16, one, 0)

    def send_near(self):
        p = self.p
        into = self.dst.at[p.s, :, pl.ds(p.col, HALF)]

        def one(i, _):
            to = p.near(i)
            self.send(self.src.at[to], into, 1, self.direct.at[p.x], to, p.r)
            return 0

        pltpu.make_async_copy(self.src.at[p.s], into, self.direct.at[p.x]).start()
        lax.fori_loop(1, 16, one, 0)

    def far_band(self, k, col):
        slot = self.p.far(k)
        return self.dst.at[slot, :, pl.ds(col, HALF)], slot

    def near_bands(self, g, col):
        x = lax.rem(self.p.x + hop_order(g), 4)
        return self.dst.at[pl.ds(self.p.shard(x, self.p.h, 0), 4), :, pl.ds(col, HALF)], x

    def relay(self, k):
        p = self.p
        at, slot = self.far_band(k, p.col)
        pltpu.make_async_copy(at, at, self.relayed.at[slot]).wait()

        @pl.when(p.hop < 3)
        def _():
            self.send(at, at, 2, self.relayed.at[slot], p.s, p.after)

        self.send(at, at, 3, self.pair_relayed.at[slot], p.s, p.partner)

    def pass_near(self, g):
        p = self.p
        at, x = self.near_bands(g, p.col)
        pltpu.make_async_copy(at, at, self.direct.at[x]).wait()
        self.send(at, at, 4, self.pair_direct.at[x], p.s, p.partner)

    def gather(self):
        p = self.p

        def step(t, _):
            k = t - LAG * p.hop

            @pl.when((k >= 0) & (k < 16))
            def _():
                self.relay(k)

            @pl.when((t >= NEAR_AT) & (t < NEAR_AT + 4))
            def _():
                self.pass_near(t - NEAR_AT)

            return 0

        lax.fori_loop(0, 16 + 3 * LAG, step, 0)

        def partner_near(g, _):
            at, x = self.near_bands(g, p.other_col)
            pltpu.make_async_copy(at, at, self.pair_direct.at[x]).wait()
            return 0

        lax.fori_loop(0, 4, partner_near, 0)

        def partner_far(k, _):
            at, slot = self.far_band(k, p.other_col)
            pltpu.make_async_copy(at, at, self.pair_relayed.at[slot]).wait()
            return 0

        lax.fori_loop(0, 16, partner_far, 0)

    def finish_sends(self):
        p = self.p

        def drain(index, slots):
            of = self.src.at[pl.ds(0, slots)]
            pltpu.make_async_copy(of, of, self.sends.at[index]).wait()

        drain(0, 4)
        drain(1, 15)

        @pl.when(p.hop < 3)
        def _():
            drain(2, 16)

        drain(3, 16)
        drain(4, 16)


def halves(value, high_ref, low_ref):
    high = value.astype(BF16)
    high_ref[...] = high
    low_ref[...] = (value - high.astype(F32)).astype(BF16)


def mul(lh, ll, rh, rl):
    dot = functools.partial(jnp.dot, preferred_element_type=F32)
    return dot(lh[...], rh[...]) + (dot(lh[...], rl[...]) + dot(ll[...], rh[...]))


def chain(x_ref, gram, q, ah, al, rh, rl, ch, cl, qh, ql):
    eye = lax.broadcasted_iota(jnp.int32, (ROWS, ROWS), 0) == lax.broadcasted_iota(
        jnp.int32, (ROWS, ROWS), 1
    )
    values = x_ref[...].reshape(ROWS, COLS)
    raw = lax.dot_general(
        values, values, (((1,), (1,)), ((), ())), preferred_element_type=F32
    )
    gram[...] = raw
    square = jnp.sum(jnp.where(eye, raw, 0.0), axis=(0, 1), keepdims=True)
    inverse = 1.0 / (jnp.sqrt(square) + 1e-07)
    gram[...] = gram[...] * inverse * inverse
    q[...] = jnp.where(eye, 1.0, 0.0)
    halves(q[...], qh, ql)

    def sweep(i, _):
        halves(gram[...], ah, al)
        poly = coef_b * gram[...] + coef_c * mul(ah, al, ah, al)
        halves(poly, rh, rl)
        q[...] = coef_a * q[...] + mul(rh, rl, qh, ql)
        halves(q[...], qh, ql)

        @pl.when(i < ITERS - 1)
        def _():
            gram[...] = coef_a * gram[...] + mul(rh, rl, ah, al)
            halves(gram[...], ch, cl)
            gram[...] = coef_a * gram[...] + mul(ch, cl, rh, rl)

        return 0

    lax.fori_loop(0, ITERS, sweep, 0)
    return inverse * jnp.sqrt(F32(max(ROWS, COLS)))


def kernel(
    mom, grad, new_mom, update, mv, gv, nv, sb, sf, xb, yb, yf, ob,
    gram, q, ah, al, rh, rl, ch, cl, qh, ql,
    load_sem, store_sem, direct, relayed, pair_direct, pair_relayed, sends,
):
    p = Place()
    greet(p)

    def load(index, src, dst, col):
        return pltpu.make_async_copy(
            src.at[:, :, pl.ds(col, HALF)],
            dst.at[:, :, pl.ds(col, HALF)],
            load_sem.at[index],
        )

    loads = [
        load(0, mom, mv, p.col),
        load(1, grad, gv, p.col),
        load(2, mom, mv, p.other_col),
        load(3, grad, gv, p.other_col),
    ]
    for copy in loads:
        copy.start()
    loads[0].wait()
    loads[1].wait()

    def momentum(e, col):
        cols = pl.ds(col, HALF)
        g = gv[e, :, cols].astype(F32)
        n = (0.95 * mv[e, :, cols].astype(F32) + g).astype(BF16)
        nv[e, :, cols] = n
        return n, g

    def blend(e, _):
        n, g = momentum(e, p.col)
        sb[e] = (g + 0.95 * n.astype(F32)).astype(BF16)
        return 0

    def blend_far(e, _):
        cols = pl.ds(p.part, PART)
        g = gv[e, :, cols].astype(F32)
        n = (0.95 * mv[e, :, cols].astype(F32) + g).astype(BF16)
        sf[e] = (g + 0.95 * n.astype(F32)).astype(BF16)
        return 0

    lax.fori_loop(0, EXPERTS, blend, 0)
    loads[2].wait()
    loads[3].wait()
    lax.fori_loop(0, EXPERTS, blend_far, 0)
    await_greetings(p)

    def exchange(phase, src, far_src, dst):
        return Exchange(
            p, src, far_src, dst, direct.at[phase], relayed.at[phase],
            pair_direct.at[phase], pair_relayed.at[phase], sends.at[phase],
        )

    inward = exchange(0, sb, sf, xb)
    inward.send_across()
    inward.send_near()

    def rest(e, _):
        momentum(e, p.other_col)
        return 0

    lax.fori_loop(0, EXPERTS, rest, 0)
    store = pltpu.make_async_copy(nv, new_mom, store_sem.at[0])
    store.start()
    inward.gather()

    factor = chain(xb, gram, q, ah, al, rh, rl, ch, cl, qh, ql)

    dot = functools.partial(jnp.dot, preferred_element_type=F32)

    def product(h, cols, width):
        rows = [pl.ds(pl.multiple_of(x * 128 + h * 64, 64), 64) for x in range(4)]
        high = jnp.concatenate([qh[i, :] for i in rows], 0)
        low = jnp.concatenate([ql[i, :] for i in rows], 0)
        values = xb[:, :, pl.ds(cols, width)].reshape(ROWS, width)
        return ((dot(high, values) + dot(low, values)) * factor).astype(BF16)

    outward = exchange(1, yb, yf, ob)
    part = product(1 - p.h, p.part, PART).reshape(4, 4, BAND, PART)
    for x in range(4):
        yf[pl.ds(p.shard(x, 1 - p.h, 0), 4)] = part[x]
    outward.send_across()
    part = product(p.h, p.col, HALF).reshape(4, 4, BAND, HALF)
    for x in range(4):
        yb[pl.ds(p.shard(x, p.h, 0), 4)] = part[x]
    outward.send_near()
    outward.gather()
    out = pltpu.make_async_copy(ob, update, store_sem.at[1])
    out.start()
    inward.finish_sends()
    outward.finish_sends()
    store.wait()
    out.wait()


def shards(momentum, gradient):
    whole = (EXPERTS, BAND, COLS)
    dma = pltpu.SemaphoreType.DMA
    square = (ROWS, ROWS)
    return pl.pallas_call(
        kernel,
        out_shape=(
            jax.ShapeDtypeStruct(whole, BF16),
            jax.ShapeDtypeStruct(whole, BF16),
        ),
        in_specs=[pl.BlockSpec(memory_space=pl.ANY)] * 2,
        out_specs=[pl.BlockSpec(memory_space=pl.ANY)] * 2,
        scratch_shapes=[
            pltpu.VMEM(whole, BF16),
            pltpu.VMEM(whole, BF16),
            pltpu.VMEM(whole, BF16),
            pltpu.VMEM((EXPERTS, BAND, HALF), BF16),
            pltpu.VMEM((EXPERTS, BAND, PART), BF16),
            pltpu.VMEM(whole, BF16),
            pltpu.VMEM((EXPERTS, BAND, HALF), BF16),
            pltpu.VMEM((EXPERTS, BAND, PART), BF16),
            pltpu.VMEM(whole, BF16),
            pltpu.VMEM(square, F32),
            pltpu.VMEM(square, F32),
        ]
        + [pltpu.VMEM(square, BF16)] * 8
        + [
            dma((4,)),
            dma((2,)),
            dma((2, 4)),
            dma((2, 32)),
            dma((2, 4)),
            dma((2, 32)),
            dma((2, 5)),
        ],
        compiler_params=pltpu.CompilerParams(
            collective_id=0,
            has_side_effects=True,
            vmem_limit_bytes=48 * 1024 * 1024,
        ),
    )(momentum, gradient)


def solution(mesh):
    return jax.shard_map(
        shards,
        mesh=mesh,
        in_specs=(P(None, "shard", None), P(None, "shard", None)),
        out_specs=(P(None, "shard", None), P(None, "shard", None)),
        check_vma=False,
    )
```

```python
import functools

import jax
import jax.numpy as jnp
from jax import lax
from jax.experimental import pallas as pl
from jax.experimental.pallas import tpu as pltpu
from jax.sharding import PartitionSpec as P

ROWS = 512
COLS = 2048
ITERS = 5
EXPERTS = 32

coef_a = 3.4445
coef_b = -4.775
coef_c = 2.0315

MESH = pl.DeviceIdType.MESH
F32 = jnp.float32
BF16 = jnp.bfloat16

BAND = ROWS // 32
HALF = COLS // 2
PART = COLS // 8
LAG = 4
NEAR_AT = 13


def hop_order(step):
    return lax.rem(step + step // 2 - 2 * (step // 3), 4)


class Place:
    def __init__(self):
        self.s = lax.axis_index("shard")
        self.r = lax.axis_index("rep")
        self.x = self.s // 8
        self.h = (self.s // 4) % 2
        self.y = self.s % 4
        self.zl = self.r // 2
        self.c = self.r % 2
        self.partner = self.zl * 2 + 1 - self.c
        self.hop = (1 - self.c) * (3 - self.zl) + self.c * self.zl
        self.before = self.r + 2 - 4 * self.c
        self.after = self.r - 2 + 4 * self.c
        self.collector = 7 * (self.r // 4)
        self.collects = (7 - self.r) // 7 + self.r // 7
        self.first = 6 - 5 * (self.zl // 2)
        self.col = pl.multiple_of(self.c * HALF, HALF)
        self.other_col = pl.multiple_of((1 - self.c) * HALF, HALF)
        self.part = pl.multiple_of(self.r * PART, PART)

    def shard(self, x, h, y):
        return x * 8 + h * 4 + y

    def far(self, i):
        x = lax.rem(self.x + hop_order(i // 4), 4)
        y = lax.rem(self.y + hop_order(i % 4), 4)
        return self.shard(x, 1 - self.h, y)

    def near(self, i):
        x = lax.rem(self.x + hop_order(i // 4), 4)
        y = lax.rem(self.y + hop_order(i % 4), 4)
        return self.shard(x, self.h, y)


def signal(semaphore, s, r):
    pl.semaphore_signal(semaphore, inc=1, device_id=(s, r), device_id_type=MESH)


def greet(p):
    barrier = pltpu.get_barrier_semaphore()

    def near(i, _):
        signal(barrier, p.near(i), p.r)
        return 0

    def across(i, _):
        signal(barrier, p.far(i), 7 * p.c)
        return 0

    @pl.when(p.hop == 0)
    def _():
        lax.fori_loop(0, 16, across, 0)

    @pl.when(p.collects == 0)
    def _():
        signal(barrier, p.s, p.collector)

    lax.fori_loop(1, 16, near, 0)
    signal(barrier, p.s, p.partner)

    @pl.when(p.hop > 0)
    def _():
        signal(barrier, p.s, p.before)


def await_greetings(p, told):
    pl.semaphore_wait(pltpu.get_barrier_semaphore(), 15 + 1 + 1 - p.hop // 3 + 19 * p.collects)

    @pl.when(p.collects == 1)
    def _():
        for i in range(1, 4):
            signal(told, p.s, p.collector + i - 2 * i * (p.r // 7))

    @pl.when(p.collects == 0)
    def _():
        pl.semaphore_wait(told, 1)


class Exchange:
    def __init__(self, p, src, far_src, dst, direct, relayed, pair_direct, pair_relayed, sends):
        self.p, self.src, self.far_src, self.dst = p, src, far_src, dst
        self.direct, self.relayed = direct, relayed
        self.pair_direct, self.pair_relayed = pair_direct, pair_relayed
        self.sends = sends

    def send(self, src, dst, send_sem, recv_sem, s, r):
        pltpu.make_async_remote_copy(
            src_ref=src,
            dst_ref=dst,
            send_sem=self.sends.at[send_sem],
            recv_sem=recv_sem,
            device_id=(s, r),
            device_id_type=MESH,
        ).start()

    def send_across(self):
        p = self.p

        def one(i, _):
            to = p.far(i)
            into = self.dst.at[p.s, :, pl.ds(p.part, PART)]
            self.send(self.far_src.at[to], into, 0, self.relayed.at[p.s], to, p.first)
            return 0

        lax.fori_loop(0, 16, one, 0)

    def send_near(self):
        p = self.p
        into = self.dst.at[p.s, :, pl.ds(p.col, HALF)]

        def one(i, _):
            to = p.near(i)
            self.send(self.src.at[to], into, 1, self.direct.at[p.x], to, p.r)
            return 0

        pltpu.make_async_copy(self.src.at[p.s], into, self.direct.at[p.x]).start()
        lax.fori_loop(1, 16, one, 0)

    def far_band(self, k, col):
        slot = self.p.far(k)
        return self.dst.at[slot, :, pl.ds(col, HALF)], slot

    def near_bands(self, g, col):
        x = lax.rem(self.p.x + hop_order(g), 4)
        return self.dst.at[pl.ds(self.p.shard(x, self.p.h, 0), 4), :, pl.ds(col, HALF)], x

    def relay(self, k):
        p = self.p
        at, slot = self.far_band(k, p.col)
        pltpu.make_async_copy(at, at, self.relayed.at[slot]).wait()

        @pl.when(p.hop < 3)
        def _():
            self.send(at, at, 2, self.relayed.at[slot], p.s, p.after)

        self.send(at, at, 3, self.pair_relayed.at[slot], p.s, p.partner)

    def pass_near(self, g):
        p = self.p
        at, x = self.near_bands(g, p.col)
        pltpu.make_async_copy(at, at, self.direct.at[x]).wait()
        self.send(at, at, 4, self.pair_direct.at[x], p.s, p.partner)

    def gather(self):
        p = self.p

        def step(t, _):
            k = t - LAG * p.hop

            @pl.when((k >= 0) & (k < 16))
            def _():
                self.relay(k)

            @pl.when((t >= NEAR_AT) & (t < NEAR_AT + 4))
            def _():
                self.pass_near(t - NEAR_AT)

            return 0

        lax.fori_loop(0, 16 + 3 * LAG, step, 0)

        def partner_near(g, _):
            at, x = self.near_bands(g, p.other_col)
            pltpu.make_async_copy(at, at, self.pair_direct.at[x]).wait()
            return 0

        lax.fori_loop(0, 4, partner_near, 0)

        def partner_far(k, _):
            at, slot = self.far_band(k, p.other_col)
            pltpu.make_async_copy(at, at, self.pair_relayed.at[slot]).wait()
            return 0

        lax.fori_loop(0, 16, partner_far, 0)

    def finish_sends(self):
        p = self.p

        def drain(index, slots):
            of = self.src.at[pl.ds(0, slots)]
            pltpu.make_async_copy(of, of, self.sends.at[index]).wait()

        drain(0, 4)
        drain(1, 15)

        @pl.when(p.hop < 3)
        def _():
            drain(2, 16)

        drain(3, 16)
        drain(4, 16)


def chain(x_ref, gram, q, ah, al, rh, rl, ch, cl, qh, ql, q2h, q2l):
    half = ROWS // 2
    s0, s1, both = slice(0, half), slice(half, ROWS), slice(0, ROWS)
    blocks = ((s0, s1), (s0, s0), (s1, s1))
    dot = functools.partial(jnp.dot, preferred_element_type=F32)

    def eye(rows, cols):
        shape = (rows.stop - rows.start, cols.stop - cols.start)
        row = lax.broadcasted_iota(jnp.int32, shape, 0) + rows.start
        return row == lax.broadcasted_iota(jnp.int32, shape, 1) + cols.start

    def put(value, rows, cols, pair):
        def split(value, at):
            high = value.astype(BF16)
            pair[0][at] = high
            pair[1][at] = (value - high.astype(F32)).astype(BF16)

        split(value, (rows, cols))
        if cols.stop > rows.stop:
            split(value[:, half - cols.start :].T, (s1, s0))

    def product(left, right, finish, into, keep=None):
        for rows, cols in blocks:
            a, b = left[0][rows, :], left[1][rows, :]
            c, d = right[0][:, cols], right[1][:, cols]
            value = finish(dot(a, c) + (dot(a, d) + dot(b, c)), rows, cols)
            if keep is not None:
                keep[rows, cols] = value
            put(value, rows, cols, into)

    def plus(ref):
        return lambda value, rows, cols: coef_a * ref[rows, cols] + value

    def poly(value, rows, cols):
        return coef_b * gram[rows, cols] + coef_c * value

    values = x_ref[...].reshape(ROWS, COLS)
    nt = (((1,), (1,)), ((), ()))
    square = 0.0
    for rows, cols in blocks:
        raw = lax.dot_general(values[rows], values[cols], nt, preferred_element_type=F32)
        gram[rows, cols] = raw
        if cols.start <= rows.start:
            square += jnp.sum(jnp.where(eye(rows, cols), raw, 0.0), axis=(0, 1), keepdims=True)
    inverse = 1.0 / (jnp.sqrt(square) + 1e-07)
    A, R, C = (ah, al), (rh, rl), (ch, cl)
    for rows, cols in blocks:
        value = gram[rows, cols] * inverse * inverse
        gram[rows, cols] = value
        put(value, rows, cols, A)
    now, later = (qh, ql), (q2h, q2l)
    for i in range(ITERS):
        if i == 0:
            for rows, cols in blocks:
                a, b = ah[rows, :], al[rows, :]
                c, d = ah[:, cols], al[:, cols]
                value = poly(dot(a, c) + (dot(a, d) + dot(b, c)), rows, cols)
                put(value, rows, cols, R)
                value = jnp.where(eye(rows, cols), coef_a, 0.0) + value
                q[rows, cols] = value
                put(value, rows, cols, now)
        else:
            product(A, A, poly, R)
        if i < ITERS - 1:
            product(R, A, plus(gram), C, gram)
        if i > 0:
            product(R, now, plus(q), later, q)
            now, later = later, now
        if i < ITERS - 1:
            product(C, R, plus(gram), A, gram)

    return inverse * jnp.sqrt(F32(max(ROWS, COLS)))


def kernel(
    mom, grad, new_mom, update, mv, gv, sb, sf, xb, yb, yf,
    gram, q, ah, al, rh, rl, ch, cl, qh, ql, q2h, q2l,
    load_sem, told, direct, relayed, pair_direct, pair_relayed, sends,
):
    p = Place()
    loads = [
        pltpu.make_async_copy(src, dst, load_sem.at[i])
        for i, (src, dst) in enumerate(((mom, mv), (grad, gv)))
    ]
    for copy in loads:
        copy.start()
    greet(p)
    for copy in loads:
        copy.wait()

    def momentum(e, cols):
        g = gv[e, :, cols].astype(F32)
        return (0.95 * mv[e, :, cols].astype(F32) + g).astype(BF16), g

    def blend(e, cols):
        n, g = momentum(e, cols)
        return (g + 0.95 * n.astype(F32)).astype(BF16)

    def blend_far(i, _):
        e = p.far(i)
        sf[e] = blend(e, pl.ds(p.part, PART))
        return 0

    def blend_near(i, _):
        e = p.near(i)
        sb[e] = blend(e, pl.ds(p.col, HALF))
        return 0

    lax.fori_loop(0, 16, blend_far, 0)
    lax.fori_loop(0, 16, blend_near, 0)
    await_greetings(p, told)

    def exchange(phase, src, far_src, dst):
        return Exchange(
            p, src, far_src, dst, direct.at[phase], relayed.at[phase],
            pair_direct.at[phase], pair_relayed.at[phase], sends.at[phase],
        )

    inward = exchange(0, sb, sf, xb)
    inward.send_across()
    inward.send_near()

    def whole_momentum(e, _):
        new_mom[e], _ = momentum(e, slice(None))
        return 0

    lax.fori_loop(0, EXPERTS, whole_momentum, 0)
    inward.gather()

    factor = chain(xb, gram, q, ah, al, rh, rl, ch, cl, qh, ql, q2h, q2l)

    dot = functools.partial(jnp.dot, preferred_element_type=F32)

    def product(h, cols, width):
        rows = [pl.ds(pl.multiple_of(x * 128 + h * 64, 64), 64) for x in range(4)]
        high = jnp.concatenate([qh[i, :] for i in rows], 0)
        low = jnp.concatenate([ql[i, :] for i in rows], 0)
        values = xb[:, :, pl.ds(cols, width)].reshape(ROWS, width)
        return ((dot(high, values) + dot(low, values)) * factor).astype(BF16)

    outward = exchange(1, yb, yf, update)
    part = product(1 - p.h, p.part, PART).reshape(4, 4, BAND, PART)
    for x in range(4):
        yf[pl.ds(p.shard(x, 1 - p.h, 0), 4)] = part[x]
    outward.send_across()
    part = product(p.h, p.col, HALF).reshape(4, 4, BAND, HALF)
    for x in range(4):
        yb[pl.ds(p.shard(x, p.h, 0), 4)] = part[x]
    outward.send_near()
    outward.gather()
    inward.finish_sends()
    outward.finish_sends()


def shards(momentum, gradient):
    whole = (EXPERTS, BAND, COLS)
    dma = pltpu.SemaphoreType.DMA
    square = (ROWS, ROWS)
    return pl.pallas_call(
        kernel,
        out_shape=(
            jax.ShapeDtypeStruct(whole, BF16),
            jax.ShapeDtypeStruct(whole, BF16),
        ),
        in_specs=[pl.BlockSpec(memory_space=pl.ANY)] * 2,
        out_specs=[pl.BlockSpec(memory_space=pltpu.VMEM)] * 2,
        scratch_shapes=[
            pltpu.VMEM(whole, BF16),
            pltpu.VMEM(whole, BF16),
            pltpu.VMEM((EXPERTS, BAND, HALF), BF16),
            pltpu.VMEM((EXPERTS, BAND, PART), BF16),
            pltpu.VMEM(whole, BF16),
            pltpu.VMEM((EXPERTS, BAND, HALF), BF16),
            pltpu.VMEM((EXPERTS, BAND, PART), BF16),
            pltpu.VMEM(square, F32),
            pltpu.VMEM(square, F32),
        ]
        + [pltpu.VMEM(square, BF16)] * 10
        + [
            dma((2,)),
            pltpu.SemaphoreType.REGULAR,
            dma((2, 4)),
            dma((2, 32)),
            dma((2, 4)),
            dma((2, 32)),
            dma((2, 5)),
        ],
        compiler_params=pltpu.CompilerParams(
            collective_id=0,
            has_side_effects=True,
            vmem_limit_bytes=48 * 1024 * 1024,
        ),
    )(momentum, gradient)


def solution(mesh):
    return jax.shard_map(
        shards,
        mesh=mesh,
        in_specs=(P(None, "shard", None), P(None, "shard", None)),
        out_specs=(P(None, "shard", None), P(None, "shard", None)),
        check_vma=False,
    )
```

```python
import functools

import jax
import jax.numpy as jnp
from jax import lax
from jax.experimental import pallas as pl
from jax.experimental.pallas import tpu as pltpu
from jax.sharding import PartitionSpec as P

ROWS = 512
COLS = 2048
ITERS = 5
EXPERTS = 32

coef_a = 3.4445
coef_b = -4.775
coef_c = 2.0315

MESH = pl.DeviceIdType.MESH
F32 = jnp.float32
BF16 = jnp.bfloat16

BAND = ROWS // 32
HALF = COLS // 2
PART = COLS // 4
LAG = 4
NEAR_AT = 13


def hop_order(step):
    return lax.rem(step + step // 2 - 2 * (step // 3), 4)


class Place:
    def __init__(self):
        self.s = lax.axis_index("shard")
        self.r = lax.axis_index("rep")
        self.x = self.s // 8
        self.h = (self.s // 4) % 2
        self.y = self.s % 4
        self.zl = self.r // 2
        self.c = self.r % 2
        self.partner = self.zl * 2 + 1 - self.c
        self.hop = (1 - self.c) * (3 - self.zl) + self.c * self.zl
        self.before = self.r + 2 - 4 * self.c
        self.after = self.r - 2 + 4 * self.c
        self.end = self.zl // 3
        self.sends_far = (self.zl == 0) | (self.zl == 3)
        self.collects = (7 - self.r) // 7 + self.r // 7
        self.first = 6 - 5 * self.end
        self.col = pl.multiple_of(self.c * HALF, HALF)
        self.other_col = pl.multiple_of((1 - self.c) * HALF, HALF)
        self.part = pl.multiple_of(self.end * HALF + self.c * PART, PART)

    def shard(self, x, h, y):
        return x * 8 + h * 4 + y

    def around(self, i):
        return lax.rem(self.x + hop_order(i // 4), 4), lax.rem(self.y + hop_order(i % 4), 4)

    def far(self, i):
        x, y = self.around(i)
        return self.shard(x, 1 - self.h, y)

    def near(self, i):
        x, y = self.around(i)
        return self.shard(x, self.h, y)


def signal(semaphore, s, r):
    pl.semaphore_signal(semaphore, inc=1, device_id=(s, r), device_id_type=MESH)


def greet(p):
    barrier = pltpu.get_barrier_semaphore()

    def near(i, _):
        signal(barrier, p.near(i), p.r)
        return 0

    def across(i, _):
        signal(barrier, p.far(i), 7 * p.c)
        return 0

    @pl.when(p.hop == 0)
    def _():
        lax.fori_loop(0, 16, across, 0)

    lax.fori_loop(1, 16, near, 0)
    signal(barrier, p.s, p.partner)

    @pl.when(p.hop > 0)
    def _():
        signal(barrier, p.s, p.before)


def await_greetings(p, told):
    pl.semaphore_wait(pltpu.get_barrier_semaphore(), 15 + 1 + 1 - p.hop // 3 + 16 * p.collects)

    @pl.when(p.collects == 1)
    def _():
        signal(told, p.s, p.partner)

    @pl.when(p.sends_far & (p.collects == 0))
    def _():
        pl.semaphore_wait(told, 1)


class Exchange:
    def __init__(self, p, near_first, src, far_src, dst, direct, relayed, pair_direct, pair_relayed, sends):
        self.p, self.near_first = p, near_first
        self.src, self.far_src, self.dst = src, far_src, dst
        self.direct, self.relayed = direct, relayed
        self.pair_direct, self.pair_relayed = pair_direct, pair_relayed
        self.sends = sends

    def slot(self, x, h, y, far):
        return 16 * far + x * 4 + y if self.near_first else self.p.shard(x, h, y)

    def send(self, src, dst, send_sem, recv_sem, s, r):
        pltpu.make_async_remote_copy(
            src_ref=src,
            dst_ref=dst,
            send_sem=self.sends.at[send_sem],
            recv_sem=recv_sem,
            device_id=(s, r),
            device_id_type=MESH,
        ).start()

    def send_across(self):
        p = self.p
        into = self.dst.at[self.slot(p.x, p.h, p.y, 1), :, pl.ds(p.part, PART)]

        def one(i, _):
            x, y = p.around(i)
            done = self.relayed.at[p.x * 4 + p.y]
            self.send(self.far_src.at[x * 4 + y], into, 0, done, p.far(i), p.first)
            return 0

        lax.fori_loop(0, 16, one, 0)

    def send_near(self):
        p = self.p
        into = self.dst.at[self.slot(p.x, p.h, p.y, 0), :, pl.ds(p.col, HALF)]

        def one(i, _):
            x, y = p.around(i)
            self.send(self.src.at[x * 4 + y], into, 1, self.direct.at[p.x], p.near(i), p.r)
            return 0

        pltpu.make_async_copy(self.src.at[p.x * 4 + p.y], into, self.direct.at[p.x]).start()
        lax.fori_loop(1, 16, one, 0)

    def far_band(self, k, col):
        x, y = self.p.around(k)
        return self.dst.at[self.slot(x, 1 - self.p.h, y, 1), :, pl.ds(col, HALF)], x * 4 + y

    def near_bands(self, g, col):
        x = lax.rem(self.p.x + hop_order(g), 4)
        return self.dst.at[pl.ds(self.slot(x, self.p.h, 0, 0), 4), :, pl.ds(col, HALF)], x

    def relay(self, k):
        p = self.p
        at, band = self.far_band(k, p.col)
        pltpu.make_async_copy(at, at, self.relayed.at[band]).wait()

        @pl.when(p.hop < 3)
        def _():
            self.send(at, at, 2, self.relayed.at[band], p.s, p.after)

        self.send(at, at, 3, self.pair_relayed.at[band], p.s, p.partner)

    def pass_near(self, g):
        p = self.p
        at, x = self.near_bands(g, p.col)
        pltpu.make_async_copy(at, at, self.direct.at[x]).wait()
        self.send(at, at, 4, self.pair_direct.at[x], p.s, p.partner)

    def gather(self, with_near=lambda: None):
        p = self.p

        def step(t, _):
            k = t - LAG * p.hop

            @pl.when((k >= 0) & (k < 16))
            def _():
                self.relay(k)

            @pl.when((t >= NEAR_AT) & (t < NEAR_AT + 4))
            def _():
                self.pass_near(t - NEAR_AT)

            return 0

        lax.fori_loop(0, 16 + 3 * LAG, step, 0)

        def partner_near(g, _):
            at, x = self.near_bands(g, p.other_col)
            pltpu.make_async_copy(at, at, self.pair_direct.at[x]).wait()
            return 0

        lax.fori_loop(0, 4, partner_near, 0)
        with_near()

        def partner_far(k, _):
            at, band = self.far_band(k, p.other_col)
            pltpu.make_async_copy(at, at, self.pair_relayed.at[band]).wait()
            return 0

        lax.fori_loop(0, 16, partner_far, 0)

    def finish_sends(self):
        p = self.p

        def drain(index, slots):
            of = self.src.at[pl.ds(0, slots)]
            pltpu.make_async_copy(of, of, self.sends.at[index]).wait()

        @pl.when(p.sends_far)
        def _():
            drain(0, 8)

        drain(1, 15)

        @pl.when(p.hop < 3)
        def _():
            drain(2, 16)

        drain(3, 16)
        drain(4, 16)


def gram_block(x_ref, rows, cols):
    left, right = (
        x_ref[at.start // BAND : at.stop // BAND].reshape(ROWS // 2, COLS) for at in (rows, cols)
    )
    nt = (((1,), (1,)), ((), ()))
    return lax.dot_general(left, right, nt, preferred_element_type=F32)


def chain(x_ref, gram, q, ah, al, rh, rl, ch, cl, qh, ql, q2h, q2l):
    half = ROWS // 2
    s0, s1, both = slice(0, half), slice(half, ROWS), slice(0, ROWS)
    blocks = ((s0, s1), (s0, s0), (s1, s1))
    dot = functools.partial(jnp.dot, preferred_element_type=F32)

    def eye(rows, cols):
        shape = (rows.stop - rows.start, cols.stop - cols.start)
        row = lax.broadcasted_iota(jnp.int32, shape, 0) + rows.start
        return row == lax.broadcasted_iota(jnp.int32, shape, 1) + cols.start

    def put(value, rows, cols, pair):
        def split(value, at):
            high = value.astype(BF16)
            pair[0][at] = high
            pair[1][at] = (value - high.astype(F32)).astype(BF16)

        split(value, (rows, cols))
        if cols.stop > rows.stop:
            split(value[:, half - cols.start :].T, (s1, s0))

    def product(left, right, finish, into, keep=None):
        for rows, cols in blocks:
            a, b = left[0][rows, :], left[1][rows, :]
            c, d = right[0][:, cols], right[1][:, cols]
            value = finish(dot(a, c) + (dot(a, d) + dot(b, c)), rows, cols)
            if keep is not None:
                keep[rows, cols] = value
            put(value, rows, cols, into)

    def plus(ref):
        return lambda value, rows, cols: coef_a * ref[rows, cols] + value

    def poly(value, rows, cols):
        return coef_b * gram[rows, cols] + coef_c * value

    for rows, cols in blocks:
        if (rows, cols) != (s0, s0):
            gram[rows, cols] = gram_block(x_ref, rows, cols)
    square = sum(
        jnp.sum(jnp.where(eye(rows, rows), gram[rows, rows], 0.0), axis=(0, 1), keepdims=True)
        for rows in (s0, s1)
    )
    inverse = 1.0 / (jnp.sqrt(square) + 1e-07)
    A, R, C = (ah, al), (rh, rl), (ch, cl)
    for rows, cols in blocks:
        value = gram[rows, cols] * inverse * inverse
        gram[rows, cols] = value
        put(value, rows, cols, A)
    now, later = (qh, ql), (q2h, q2l)
    for i in range(ITERS):
        if i == 0:
            for rows, cols in blocks:
                a, b = ah[rows, :], al[rows, :]
                c, d = ah[:, cols], al[:, cols]
                value = poly(dot(a, c) + (dot(a, d) + dot(b, c)), rows, cols)
                put(value, rows, cols, R)
                value = jnp.where(eye(rows, cols), coef_a, 0.0) + value
                q[rows, cols] = value
                put(value, rows, cols, now)
        else:
            product(A, A, poly, R)
        if i < ITERS - 1:
            product(R, A, plus(gram), C, gram)
        if i > 0:
            product(R, now, plus(q), later, q)
            now, later = later, now
        if i < ITERS - 1:
            product(C, R, plus(gram), A, gram)

    return inverse * jnp.sqrt(F32(max(ROWS, COLS)))


def kernel(
    mom, grad, new_mom, update, mv, gv, sb, sf, xb, yb, yf,
    gram, q, ah, al, rh, rl, ch, cl, qh, ql, q2h, q2l,
    load_sem, told, direct, relayed, pair_direct, pair_relayed, sends,
):
    p = Place()

    def loads(j):
        cols = pl.ds(pl.multiple_of(lax.rem(p.part + j * PART, COLS), PART), PART)
        return [
            pltpu.make_async_copy(src.at[:, :, cols], dst.at[:, :, cols], load_sem.at[2 * j + i])
            for i, (src, dst) in enumerate(((mom, mv), (grad, gv)))
        ]

    pending = [loads(j) for j in range(4)]
    for copies in pending:
        for copy in copies:
            copy.start()
    greet(p)
    for copy in pending[0]:
        copy.wait()

    def momentum(e, cols):
        g = gv[e, :, cols].astype(F32)
        return (0.95 * mv[e, :, cols].astype(F32) + g).astype(BF16), g

    def blend(e, cols):
        n, g = momentum(e, cols)
        return (g + 0.95 * n.astype(F32)).astype(BF16)

    def blend_far(i, _):
        x, y = p.around(i)
        sf[x * 4 + y] = blend(p.far(i), pl.ds(p.part, PART))
        return 0

    def blend_near(i, _):
        x, y = p.around(i)
        sb[x * 4 + y] = blend(p.near(i), pl.ds(p.col, HALF))
        return 0

    def exchange(phase, src, far_src, dst):
        return Exchange(
            p, phase == 0, src, far_src, dst, direct.at[phase], relayed.at[phase],
            pair_direct.at[phase], pair_relayed.at[phase], sends.at[phase],
        )

    inward = exchange(0, sb, sf, xb)

    @pl.when(p.sends_far)
    def _():
        lax.fori_loop(0, 16, blend_far, 0)

    await_greetings(p, told)

    @pl.when(p.sends_far)
    def _():
        inward.send_across()

    for copies in pending[1:]:
        for copy in copies:
            copy.wait()
    lax.fori_loop(0, 16, blend_near, 0)
    inward.send_near()

    def whole_momentum(e, _):
        new_mom[e], _ = momentum(e, slice(None))
        return 0

    lax.fori_loop(0, EXPERTS, whole_momentum, 0)

    half = ROWS // 2
    near_rows, far_rows = slice(0, half), slice(half, ROWS)

    def near_gram():
        gram[near_rows, near_rows] = gram_block(xb, near_rows, near_rows)

    inward.gather(near_gram)

    factor = chain(xb, gram, q, ah, al, rh, rl, ch, cl, qh, ql, q2h, q2l)

    dot = functools.partial(jnp.dot, preferred_element_type=F32)

    def product(rows, cols, width):
        values = xb[:, :, pl.ds(cols, width)].reshape(ROWS, width)
        out = (dot(qh[rows, :], values) + dot(ql[rows, :], values)) * factor
        return out.astype(BF16).reshape(16, BAND, width)

    outward = exchange(1, yb, yf, update)

    @pl.when(p.sends_far)
    def _():
        yf[...] = product(far_rows, p.part, PART)
        outward.send_across()

    yb[...] = product(near_rows, p.col, HALF)
    outward.send_near()
    outward.gather()
    inward.finish_sends()
    outward.finish_sends()


def write_out(first, second, first_out, second_out, sem):
    copies = [
        pltpu.make_async_copy(src.at[pl.ds(8 * j, 8)], dst.at[pl.ds(8 * j, 8)], sem.at[i, j])
        for j in range(4)
        for i, (src, dst) in enumerate(((first, first_out), (second, second_out)))
    ]
    for copy in copies:
        copy.start()
    for copy in copies:
        copy.wait()


def shards(momentum, gradient):
    whole = (EXPERTS, BAND, COLS)
    dma = pltpu.SemaphoreType.DMA
    square = (ROWS, ROWS)
    results = pl.pallas_call(
        kernel,
        out_shape=(
            jax.ShapeDtypeStruct(whole, BF16),
            jax.ShapeDtypeStruct(whole, BF16),
        ),
        in_specs=[pl.BlockSpec(memory_space=pl.ANY)] * 2,
        out_specs=[pl.BlockSpec(memory_space=pltpu.VMEM)] * 2,
        scratch_shapes=[
            pltpu.VMEM(whole, BF16),
            pltpu.VMEM(whole, BF16),
            pltpu.VMEM((16, BAND, HALF), BF16),
            pltpu.VMEM((16, BAND, PART), BF16),
            pltpu.VMEM(whole, BF16),
            pltpu.VMEM((16, BAND, HALF), BF16),
            pltpu.VMEM((16, BAND, PART), BF16),
            pltpu.VMEM(square, F32),
            pltpu.VMEM(square, F32),
        ]
        + [pltpu.VMEM(square, BF16)] * 10
        + [
            dma((8,)),
            pltpu.SemaphoreType.REGULAR,
            dma((2, 4)),
            dma((2, 16)),
            dma((2, 4)),
            dma((2, 16)),
            dma((2, 5)),
        ],
        compiler_params=pltpu.CompilerParams(
            collective_id=0,
            has_side_effects=True,
            vmem_limit_bytes=48 * 1024 * 1024,
        ),
    )(momentum, gradient)
    return pl.pallas_call(
        write_out,
        out_shape=(
            jax.ShapeDtypeStruct(whole, BF16),
            jax.ShapeDtypeStruct(whole, BF16),
        ),
        in_specs=[pl.BlockSpec(memory_space=pl.ANY)] * 2,
        out_specs=[pl.BlockSpec(memory_space=pltpu.HBM)] * 2,
        scratch_shapes=[dma((2, 4))],
        compiler_params=pltpu.CompilerParams(vmem_limit_bytes=1024 * 1024),
    )(*results)


def solution(mesh):
    return jax.shard_map(
        shards,
        mesh=mesh,
        in_specs=(P(None, "shard", None), P(None, "shard", None)),
        out_specs=(P(None, "shard", None), P(None, "shard", None)),
        check_vma=False,
    )
```

```python
import functools

import jax
import jax.numpy as jnp
from jax import lax
from jax.experimental import pallas as pl
from jax.experimental.pallas import tpu as pltpu
from jax.sharding import PartitionSpec as P

ROWS = 512
COLS = 2048
ITERS = 5
EXPERTS = 32

coef_a = 3.4445
coef_b = -4.775
coef_c = 2.0315

MESH = pl.DeviceIdType.MESH
F32 = jnp.float32
BF16 = jnp.bfloat16

BAND = ROWS // 32
HALF = COLS // 2
PART = COLS // 4
LAG = 4
NEAR_AT = 20


def hop_order(step):
    return lax.rem(step + step // 2 - 2 * (step // 3), 4)


class Place:
    def __init__(self):
        self.s = lax.axis_index("shard")
        self.r = lax.axis_index("rep")
        self.x = self.s // 8
        self.h = (self.s // 4) % 2
        self.y = self.s % 4
        self.zl = self.r // 2
        self.c = self.r % 2
        self.partner = self.zl * 2 + 1 - self.c
        self.hop = (1 - self.c) * (3 - self.zl) + self.c * self.zl
        self.before = self.r + 2 - 4 * self.c
        self.after = self.r - 2 + 4 * self.c
        self.end = self.zl // 3
        self.sends_far = (self.zl == 0) | (self.zl == 3)
        self.collects = (7 - self.r) // 7 + self.r // 7
        self.first = 6 - 5 * self.end
        self.col = pl.multiple_of(self.c * HALF, HALF)
        self.other_col = pl.multiple_of((1 - self.c) * HALF, HALF)
        self.part = pl.multiple_of(self.end * HALF + self.c * PART, PART)

    def shard(self, x, h, y):
        return x * 8 + h * 4 + y

    def around(self, i):
        return lax.rem(self.x + hop_order(i // 4), 4), lax.rem(self.y + hop_order(i % 4), 4)

    def far(self, i):
        x, y = self.around(i)
        return self.shard(x, 1 - self.h, y)

    def near(self, i):
        x, y = self.around(i)
        return self.shard(x, self.h, y)


def signal(semaphore, s, r):
    pl.semaphore_signal(semaphore, inc=1, device_id=(s, r), device_id_type=MESH)


def greet(p):
    barrier = pltpu.get_barrier_semaphore()

    def near(i, _):
        signal(barrier, p.near(i), p.r)
        return 0

    def across(i, _):
        signal(barrier, p.far(i), 7 * p.c)
        return 0

    @pl.when(p.hop == 0)
    def _():
        lax.fori_loop(0, 16, across, 0)

    lax.fori_loop(1, 16, near, 0)
    signal(barrier, p.s, p.partner)

    @pl.when(p.hop > 0)
    def _():
        signal(barrier, p.s, p.before)


def await_greetings(p, told):
    pl.semaphore_wait(pltpu.get_barrier_semaphore(), 15 + 1 + 1 - p.hop // 3 + 16 * p.collects)

    @pl.when(p.collects == 1)
    def _():
        signal(told, p.s, p.partner)

    @pl.when(p.sends_far & (p.collects == 0))
    def _():
        pl.semaphore_wait(told, 1)


class Exchange:
    def __init__(self, p, near_first, src, far_src, dst, direct, relayed, pair_direct, pair_relayed, sends):
        self.p, self.near_first = p, near_first
        self.src, self.far_src, self.dst = src, far_src, dst
        self.direct, self.relayed = direct, relayed
        self.pair_direct, self.pair_relayed = pair_direct, pair_relayed
        self.sends = sends

    def slot(self, x, h, y, far):
        return 16 * far + x * 4 + y if self.near_first else self.p.shard(x, h, y)

    def send(self, src, dst, send_sem, recv_sem, s, r):
        pltpu.make_async_remote_copy(
            src_ref=src,
            dst_ref=dst,
            send_sem=self.sends.at[send_sem],
            recv_sem=recv_sem,
            device_id=(s, r),
            device_id_type=MESH,
        ).start()

    def send_across(self):
        p = self.p
        into = self.dst.at[self.slot(p.x, p.h, p.y, 1), :, pl.ds(p.part, PART)]

        def one(i, _):
            x, y = p.around(i)
            done = self.relayed.at[p.x * 4 + p.y]
            self.send(self.far_src.at[x * 4 + y], into, 0, done, p.far(i), p.first)
            return 0

        lax.fori_loop(0, 16, one, 0)

    def send_near(self):
        p = self.p
        into = self.dst.at[self.slot(p.x, p.h, p.y, 0), :, pl.ds(p.col, HALF)]

        def one(i, _):
            x, y = p.around(i)
            self.send(self.src.at[x * 4 + y], into, 1, self.direct.at[p.x], p.near(i), p.r)
            return 0

        pltpu.make_async_copy(self.src.at[p.x * 4 + p.y], into, self.direct.at[p.x]).start()
        lax.fori_loop(1, 16, one, 0)

    def far_band(self, k, col):
        x, y = self.p.around(k)
        return self.dst.at[self.slot(x, 1 - self.p.h, y, 1), :, pl.ds(col, HALF)], x * 4 + y

    def near_bands(self, g, col):
        x = lax.rem(self.p.x + hop_order(g), 4)
        return self.dst.at[pl.ds(self.slot(x, self.p.h, 0, 0), 4), :, pl.ds(col, HALF)], x

    def relay(self, k):
        p = self.p
        at, band = self.far_band(k, p.col)
        pltpu.make_async_copy(at, at, self.relayed.at[band]).wait()

        @pl.when(p.hop < 3)
        def _():
            self.send(at, at, 2, self.relayed.at[band], p.s, p.after)

        self.send(at, at, 3, self.pair_relayed.at[band], p.s, p.partner)

    def pass_near(self, g):
        p = self.p
        at, x = self.near_bands(g, p.col)
        pltpu.make_async_copy(at, at, self.direct.at[x]).wait()
        self.send(at, at, 4, self.pair_direct.at[x], p.s, p.partner)

    def gather(self, with_near=lambda: None):
        p = self.p

        def step(t, _):
            k = t - LAG * p.hop

            @pl.when((k >= 0) & (k < 16))
            def _():
                self.relay(k)

            @pl.when((t >= NEAR_AT) & (t < NEAR_AT + 4))
            def _():
                self.pass_near(t - NEAR_AT)

            return 0

        lax.fori_loop(0, 16 + 3 * LAG, step, 0)

        def partner_near(g, _):
            at, x = self.near_bands(g, p.other_col)
            pltpu.make_async_copy(at, at, self.pair_direct.at[x]).wait()
            return 0

        lax.fori_loop(0, 4, partner_near, 0)
        with_near()

        def partner_far(k, _):
            at, band = self.far_band(k, p.other_col)
            pltpu.make_async_copy(at, at, self.pair_relayed.at[band]).wait()
            return 0

        lax.fori_loop(0, 16, partner_far, 0)

    def finish_sends(self):
        p = self.p

        def drain(index, slots):
            of = self.src.at[pl.ds(0, slots)]
            pltpu.make_async_copy(of, of, self.sends.at[index]).wait()

        @pl.when(p.sends_far)
        def _():
            drain(0, 8)

        drain(1, 15)

        @pl.when(p.hop < 3)
        def _():
            drain(2, 16)

        drain(3, 16)
        drain(4, 16)


def gram_block(x_ref, rows, cols):
    left, right = (
        x_ref[at.start // BAND : at.stop // BAND].reshape(ROWS // 2, COLS) for at in (rows, cols)
    )
    nt = (((1,), (1,)), ((), ()))
    return lax.dot_general(left, right, nt, preferred_element_type=F32)


def chain(x_ref, gram, q, ah, al, rh, rl, ch, cl, qh, ql, q2h, q2l):
    half = ROWS // 2
    s0, s1, both = slice(0, half), slice(half, ROWS), slice(0, ROWS)
    blocks = ((s0, s1), (s0, s0), (s1, s1))
    dot = functools.partial(jnp.dot, preferred_element_type=F32)

    def eye(rows, cols):
        shape = (rows.stop - rows.start, cols.stop - cols.start)
        row = lax.broadcasted_iota(jnp.int32, shape, 0) + rows.start
        return row == lax.broadcasted_iota(jnp.int32, shape, 1) + cols.start

    def put(value, rows, cols, pair):
        def split(value, at):
            high = value.astype(BF16)
            pair[0][at] = high
            pair[1][at] = (value - high.astype(F32)).astype(BF16)

        split(value, (rows, cols))
        if cols.stop > rows.stop:
            split(value[:, half - cols.start :].T, (s1, s0))

    def product(left, right, finish, into, keep=None):
        for rows, cols in blocks:
            a, b = left[0][rows, :], left[1][rows, :]
            c, d = right[0][:, cols], right[1][:, cols]
            value = finish(dot(a, c) + (dot(a, d) + dot(b, c)), rows, cols)
            if keep is not None:
                keep[rows, cols] = value
            put(value, rows, cols, into)

    def plus(ref):
        return lambda value, rows, cols: coef_a * ref[rows, cols] + value

    def poly(value, rows, cols):
        return coef_b * gram[rows, cols] + coef_c * value

    for rows, cols in blocks:
        if (rows, cols) != (s0, s0):
            gram[rows, cols] = gram_block(x_ref, rows, cols)
    square = sum(
        jnp.sum(jnp.where(eye(rows, rows), gram[rows, rows], 0.0), axis=(0, 1), keepdims=True)
        for rows in (s0, s1)
    )
    inverse = 1.0 / (jnp.sqrt(square) + 1e-07)
    A, R, C = (ah, al), (rh, rl), (ch, cl)
    for rows, cols in blocks:
        value = gram[rows, cols] * inverse * inverse
        gram[rows, cols] = value
        put(value, rows, cols, A)
    now, later = (qh, ql), (q2h, q2l)
    for i in range(ITERS):
        if i == 0:
            for rows, cols in blocks:
                a, b = ah[rows, :], al[rows, :]
                c, d = ah[:, cols], al[:, cols]
                value = poly(dot(a, c) + (dot(a, d) + dot(b, c)), rows, cols)
                put(value, rows, cols, R)
                value = jnp.where(eye(rows, cols), coef_a, 0.0) + value
                q[rows, cols] = value
                put(value, rows, cols, now)
        else:
            product(A, A, poly, R)
        if i < ITERS - 1:
            product(R, A, plus(gram), C, gram)
        if i > 0:
            product(R, now, plus(q), later, q)
            now, later = later, now
        if i < ITERS - 1:
            product(C, R, plus(gram), A, gram)

    return inverse * jnp.sqrt(F32(max(ROWS, COLS)))


def kernel(
    mom, grad, new_mom, update, mv, gv, sb, sf, xb, yb, yf,
    gram, q, ah, al, rh, rl, ch, cl, qh, ql, q2h, q2l,
    load_sem, told, direct, relayed, pair_direct, pair_relayed, sends,
):
    p = Place()

    def loads(j):
        cols = pl.ds(pl.multiple_of(lax.rem(p.part + j * PART, COLS), PART), PART)
        return [
            pltpu.make_async_copy(src.at[:, :, cols], dst.at[:, :, cols], load_sem.at[2 * j + i])
            for i, (src, dst) in enumerate(((mom, mv), (grad, gv)))
        ]

    pending = [loads(j) for j in range(4)]
    for copies in pending:
        for copy in copies:
            copy.start()
    greet(p)
    for copy in pending[0]:
        copy.wait()

    def momentum(e, cols):
        g = gv[e, :, cols].astype(F32)
        return (0.95 * mv[e, :, cols].astype(F32) + g).astype(BF16), g

    def blend(e, cols):
        n, g = momentum(e, cols)
        return (g + 0.95 * n.astype(F32)).astype(BF16)

    def blend_far(i, _):
        x, y = p.around(i)
        sf[x * 4 + y] = blend(p.far(i), pl.ds(p.part, PART))
        return 0

    def blend_near(i, _):
        x, y = p.around(i)
        sb[x * 4 + y] = blend(p.near(i), pl.ds(p.col, HALF))
        return 0

    def exchange(phase, src, far_src, dst):
        return Exchange(
            p, phase == 0, src, far_src, dst, direct.at[phase], relayed.at[phase],
            pair_direct.at[phase], pair_relayed.at[phase], sends.at[phase],
        )

    inward = exchange(0, sb, sf, xb)

    @pl.when(p.sends_far)
    def _():
        lax.fori_loop(0, 16, blend_far, 0)

    await_greetings(p, told)

    @pl.when(p.sends_far)
    def _():
        inward.send_across()

    for copies in pending[1:]:
        for copy in copies:
            copy.wait()
    lax.fori_loop(0, 16, blend_near, 0)
    inward.send_near()

    def whole_momentum(e, _):
        new_mom[e], _ = momentum(e, slice(None))
        return 0

    lax.fori_loop(0, EXPERTS, whole_momentum, 0)

    half = ROWS // 2
    near_rows, far_rows = slice(0, half), slice(half, ROWS)

    def near_gram():
        gram[near_rows, near_rows] = gram_block(xb, near_rows, near_rows)

    inward.gather(near_gram)

    factor = chain(xb, gram, q, ah, al, rh, rl, ch, cl, qh, ql, q2h, q2l)

    dot = functools.partial(jnp.dot, preferred_element_type=F32)

    def product(rows, cols, width):
        values = xb[:, :, pl.ds(cols, width)].reshape(ROWS, width)
        out = (dot(qh[rows, :], values) + dot(ql[rows, :], values)) * factor
        return out.astype(BF16).reshape(16, BAND, width)

    outward = exchange(1, yb, yf, update)

    @pl.when(p.sends_far)
    def _():
        yf[...] = product(far_rows, p.part, PART)
        outward.send_across()

    yb[...] = product(near_rows, p.col, HALF)
    outward.send_near()
    outward.gather()
    inward.finish_sends()
    outward.finish_sends()


def write_out(first, second, first_out, second_out, sem):
    copies = [
        pltpu.make_async_copy(src.at[pl.ds(8 * j, 8)], dst.at[pl.ds(8 * j, 8)], sem.at[i, j])
        for j in range(4)
        for i, (src, dst) in enumerate(((first, first_out), (second, second_out)))
    ]
    for copy in copies:
        copy.start()
    for copy in copies:
        copy.wait()


def shards(momentum, gradient):
    whole = (EXPERTS, BAND, COLS)
    dma = pltpu.SemaphoreType.DMA
    square = (ROWS, ROWS)
    results = pl.pallas_call(
        kernel,
        out_shape=(
            jax.ShapeDtypeStruct(whole, BF16),
            jax.ShapeDtypeStruct(whole, BF16),
        ),
        in_specs=[pl.BlockSpec(memory_space=pl.ANY)] * 2,
        out_specs=[pl.BlockSpec(memory_space=pltpu.VMEM)] * 2,
        scratch_shapes=[
            pltpu.VMEM(whole, BF16),
            pltpu.VMEM(whole, BF16),
            pltpu.VMEM((16, BAND, HALF), BF16),
            pltpu.VMEM((16, BAND, PART), BF16),
            pltpu.VMEM(whole, BF16),
            pltpu.VMEM((16, BAND, HALF), BF16),
            pltpu.VMEM((16, BAND, PART), BF16),
            pltpu.VMEM(square, F32),
            pltpu.VMEM(square, F32),
        ]
        + [pltpu.VMEM(square, BF16)] * 10
        + [
            dma((8,)),
            pltpu.SemaphoreType.REGULAR,
            dma((2, 4)),
            dma((2, 16)),
            dma((2, 4)),
            dma((2, 16)),
            dma((2, 5)),
        ],
        compiler_params=pltpu.CompilerParams(
            collective_id=0,
            has_side_effects=True,
            vmem_limit_bytes=48 * 1024 * 1024,
        ),
    )(momentum, gradient)
    return pl.pallas_call(
        write_out,
        out_shape=(
            jax.ShapeDtypeStruct(whole, BF16),
            jax.ShapeDtypeStruct(whole, BF16),
        ),
        in_specs=[pl.BlockSpec(memory_space=pl.ANY)] * 2,
        out_specs=[pl.BlockSpec(memory_space=pltpu.HBM)] * 2,
        scratch_shapes=[dma((2, 4))],
        compiler_params=pltpu.CompilerParams(vmem_limit_bytes=1024 * 1024),
    )(*results)


def solution(mesh):
    return jax.shard_map(
        shards,
        mesh=mesh,
        in_specs=(P(None, "shard", None), P(None, "shard", None)),
        out_specs=(P(None, "shard", None), P(None, "shard", None)),
        check_vma=False,
    )
```
